32 devices in a mesh: dp: 8 (over z, core), feat: 4 (over y, x).
Axes of the slice: x: 2, y: 2, z: 4, core: 2. Of those that a mesh axis runs over, the one named last changes fastest.
Arguments:
- bins: int32 [512, 24576], P('feat', 'dp'), may hold values from 0 to 255, as said below
- grads: float32 [8, 24576], P(None, 'dp'), may hold values from -6 to 6
- hess: float32 [8, 24576], P(None, 'dp'), may hold values from 0.05 to 1
- nodes: int32 [24576], P('dp'), may hold values from 0 to 3
- row_count: int32 [8], P('dp'), may hold values from 1 to 3072, 15360 in all
Outputs:
- best_gain: float32 [4, 512], P(None, 'feat')
The draws below stay inside these ranges and needn't reach their ends.
Inputs may be any that keep to these rules, and one draw needn't show every extreme that they name: Row slots at or beyond row_count of their dp index are padding; the counts of all dp indices add up to 5 / 8 of 24576. `bins`: each entry is a bin of its feature.
All inputs are finite; a program needn't handle non-finite values. No bound on the sum of `row_count` on one device may be relied on, other than what follows from the above.
Results may differ from the reference program's by a relative error of at most 0.0016.
Values sent between devices are 32-bit elements; how exact they have to be, the bound alone decides.
A program may use at most 64 MiB of HBM per device.

```python
import math
import jax
import jax.numpy as jnp
import numpy as np
from jax import lax

FEATS = 512
BINS = 256
OUT = 8
NODES = 4
CAP = 3072
ROWS = 24576
N_DP = 8


def draw_bins(key, part):
    weight_key = jax.random.fold_in(key, 11)
    pick_key = jax.random.fold_in(key, 23)
    powers = jax.random.randint(weight_key, (FEATS, BINS), 0, 5, dtype=jnp.int32)
    weights = jnp.left_shift(jnp.ones((FEATS, BINS), jnp.int32), powers)
    running = jnp.cumsum(weights, axis=1).astype(jnp.int32)
    totals = running[:, -1:]
    picks = jax.random.randint(pick_key, (FEATS, ROWS), 0, 1 << 30, dtype=jnp.int32)
    picks = (picks % totals).astype(jnp.int32)

    def locate(table, values):
        return jnp.searchsorted(table, values, side='right').astype(jnp.int32)
    return jax.vmap(locate)(running, picks).astype(jnp.int32)


def place_ends(values, key, least, largest):
    extent = values.shape
    place = [jax.random.randint(jax.random.fold_in(key, axis), (), 0, extent[axis]) for axis in range(len(extent))]
    values = values.at[tuple(place)].set(least)
    longest = extent.index(max(extent))
    place[longest] = (place[longest] + 1) % extent[longest]
    return values.at[tuple(place)].set(largest)


def shard_levels(own_key, dims, shards, low, largest):
    factor_of = 1.0
    for axis_at, blocks in shards:
        draws = jax.random.uniform(jax.random.fold_in(jax.random.fold_in(own_key, 6), axis_at), (blocks,), jnp.float32, low / len(shards), largest / len(shards))
        factor_of = factor_of * jnp.repeat(jnp.exp(draws), dims[axis_at] // blocks).reshape((-1,) + (1,) * (len(dims) - 1 - axis_at))
    return factor_of


def profile(amount, total, reach, lean):
    loads = [(1 << 20) // math.isqrt(standing ** lean) + 1 for standing in range(2, amount + 1)]
    spare, counts = total - reach - (amount - 1), [1] * (amount - 1)
    while spare > 0:
        movable = [i for i in range(amount - 1) if counts[i] < reach]
        pool, budget = sum([loads[i] for i in movable]), spare
        for i in movable:
            extra = min(reach - counts[i], max(1, budget * loads[i] // pool), spare)
            counts[i] = counts[i] + extra
            spare = spare - extra
    return np.array([reach] + counts)


def uneven(key, number_of, total, bound, skew):
    if number_of == 2:
        one = jax.random.randint(key, (), max(1, total - bound), min(bound, total - 1) + 1)
        return jnp.stack([one, total - one])
    lengths = jnp.asarray(profile(number_of, total, bound, skew), jnp.int32)
    couples = (number_of - 1) // 2
    giver, taker = lengths[1:1 + 2 * couples:2], lengths[2:2 + 2 * couples:2]
    room = jnp.minimum(giver - 1, bound - taker)
    shifted = jax.random.randint(jax.random.fold_in(key, 1), (couples,), 0, 1 << 20) % (room + 1)
    lengths = lengths.at[1:1 + 2 * couples:2].set(giver - shifted).at[2:2 + 2 * couples:2].set(taker + shifted)
    return lengths[jax.random.permutation(jax.random.fold_in(key, 2), number_of)]


def noise(own_key, shape, width, most, split=(), kind=jnp.bfloat16):
    factor_of = shard_levels(own_key, shape, split, -0.22, 0.18) if split else 1.0
    result = jax.random.normal(own_key, shape, jnp.float32) * width * factor_of
    return jnp.minimum(jnp.maximum(result, -most), most).astype(kind)


def setup_inputs(seed: int = 0) -> dict:
    key_of = jax.random.split(jax.random.key(seed), 6)
    return {
        "bins": draw_bins(jax.random.fold_in(key_of[5], 71), 0),
        "grads": noise(key_of[1], (OUT, ROWS), 1.0, 6.0, ((1, 8),), jnp.float32),
        "hess": jnp.clip(jnp.exp(math.log(1.0) - 2.9957323 * jax.random.uniform(key_of[2], (OUT, ROWS), jnp.float32) ** shard_levels(key_of[2], (OUT, ROWS), ((1, 8),), -0.2, 0.2)), 0.05, 1.0),
        "nodes": place_ends(jax.random.randint(key_of[3], (ROWS,), 0, NODES), jax.random.fold_in(key_of[3], 1), 0, NODES - 1).astype(jnp.int32),
        "row_count": uneven(key_of[4], N_DP, N_DP * CAP * 5 // 8, CAP, 1).astype(jnp.int32),
    }


def split_score(sums):
    shaped = sums.reshape(sums.shape[:-1] + (NODES, 2, OUT))
    grad_sum = shaped[..., 0, :]
    hess_sum = shaped[..., 1, :]
    return jnp.sum(grad_sum * grad_sum / (hess_sum + 1.0), axis=-1)


def split_gain(left_sums, all_sums):
    return split_score(left_sums) + split_score(all_sums - left_sums) - split_score(all_sums)


def reference(bins, grads, hess, nodes, row_count):
    total_rows = bins.shape[1]
    position = jnp.arange(total_rows, dtype=jnp.int32)
    is_live = (position % CAP) < row_count[position // CAP]
    member = (nodes[:, None] == jnp.arange(NODES, dtype=jnp.int32)[None, :]) & is_live[:, None]
    rounded = jnp.concatenate([grads, hess], axis=0).astype(jnp.bfloat16)
    rounded = lax.optimization_barrier(rounded)
    pair_stats = rounded.astype(jnp.float32).T
    weighted = jnp.where(member[:, :, None], pair_stats[:, None, :], jnp.zeros((), pair_stats.dtype))
    weighted = weighted.reshape(total_rows, NODES * 2 * OUT)

    def per_feature(bin_codes):
        return jax.ops.segment_sum(weighted, bin_codes, num_segments=BINS)

    histogram = lax.map(per_feature, bins)
    left_sums = jnp.cumsum(histogram, axis=1)
    all_sums = left_sums[:, -1:, :]
    split_gains = split_gain(left_sums, all_sums)
    return jnp.max(split_gains, axis=1).T
```

```python
import functools

import jax
import jax.numpy as jnp
from jax import lax
from jax.experimental import pallas as pl
from jax.experimental.pallas import tpu as pltpu
from jax.sharding import PartitionSpec as P

BINS = 256
OUT = 8
NODES = 4
PAIR = 2 * OUT
COLS = NODES * PAIR
HIGH = BINS // 2
LANES = 128
ROW_TILE = 512
OVER_LANES = (((1,), (1,)), ((), ()))


def score(sums):
    shaped = sums.reshape(NODES, PAIR, sums.shape[-1])
    grad_sum = shaped[:, :OUT, :]
    hess_sum = shaped[:, OUT:, :]
    return jnp.sum(grad_sum * grad_sum / (hess_sum + 1.0), axis=1)


def kernel(n, bins_ref, grads_ref, hess_ref, nodes_ref, count_ref, out_ref,
           bins_all, stats_all, nodes_all, weights, left_acc, gain_all,
           own_sem, bins_send, bins_recv, stats_send, stats_recv,
           nodes_send, nodes_recv, gain_send, gain_recv):
    own, rows = bins_all.shape[1:]
    me = lax.axis_index("dp")

    def partner(k):
        other, bit = 0, 1
        while bit < n:
            other = other + ((me // bit + k // bit) % 2) * bit
            bit *= 2
        return other

    def remote(src, dst, send, recv, k):
        return pltpu.make_async_remote_copy(
            src_ref=src, dst_ref=dst, send_sem=send.at[k], recv_sem=recv.at[k],
            device_id={"dp": partner(k)}, device_id_type=pl.DeviceIdType.MESH)

    def bins_copy(k):
        return remote(bins_ref.at[partner(k)], bins_all.at[k], bins_send, bins_recv, k)

    def stats_copy(k):
        return remote(stats_all.at[0], stats_all.at[k], stats_send, stats_recv, k)

    def nodes_copy(k):
        return remote(nodes_all.at[0], nodes_all.at[k], nodes_send, nodes_recv, k)

    def gain_copy(k):
        return remote(gain_all.at[0], gain_all.at[k], gain_send, gain_recv, k)

    own_copy = pltpu.make_async_copy(bins_ref.at[me], bins_all.at[0], own_sem)
    own_copy.start()
    barrier = pltpu.get_barrier_semaphore()

    @pl.loop(1, n)
    def _(k):
        pl.semaphore_signal(barrier, inc=1, device_id={"dp": partner(k)},
                            device_id_type=pl.DeviceIdType.MESH)

    slot_index = lax.broadcasted_iota(jnp.int32, (1, rows), 1)
    nodes_all[0] = jnp.where(slot_index < count_ref[0], nodes_ref[...], NODES)
    stats_all[0, :OUT] = grads_ref[...]
    stats_all[0, OUT:] = hess_ref[...]
    pl.semaphore_wait(barrier, n - 1)

    @pl.loop(1, n)
    def _(k):
        stats_copy(k).start()
        nodes_copy(k).start()
        bins_copy(k).start()

    left_acc[...] = jnp.zeros_like(left_acc)
    own_copy.wait()

    @pl.loop(0, n)
    def _(k):
        @pl.when(k > 0)
        def _():
            stats_copy(k).wait_recv()
            nodes_copy(k).wait_recv()
            bins_copy(k).wait_recv()

        stats = stats_all[k]
        label = jnp.broadcast_to(nodes_all[k], stats.shape)
        for node in range(NODES):
            weights[node * PAIR:(node + 1) * PAIR, :] = jnp.where(
                label == node, stats, 0.0).astype(jnp.bfloat16)

        @pl.loop(0, own)
        def _(feat):
            total = None
            for start in range(0, rows, ROW_TILE):
                size = min(ROW_TILE, rows - start)
                code = bins_all[k, pl.ds(feat, 1), start:start + size]
                high = (code >> 1).astype(jnp.float32).astype(jnp.bfloat16)
                low = (code & 1).astype(jnp.float32).astype(jnp.bfloat16)
                levels = lax.broadcasted_iota(jnp.int32, (HIGH, size), 0)
                levels = levels.astype(jnp.float32).astype(jnp.bfloat16)
                below = jnp.where(jnp.broadcast_to(high, (HIGH, size)) <= levels,
                                  jnp.ones((), jnp.bfloat16), jnp.zeros((), jnp.bfloat16))
                whole = weights[:, start:start + size]
                odd = whole * jnp.broadcast_to(low, (COLS, size))
                both = jnp.concatenate([whole - odd, odd], axis=0)
                part = lax.dot_general(both, below, OVER_LANES,
                                       preferred_element_type=jnp.float32)
                total = part if total is None else total + part
            left_acc[feat] = left_acc[feat] + total

    lane = lax.broadcasted_iota(jnp.int32, (COLS, HIGH), 1)
    width = gain_all.shape[-1]
    gain_lane = lax.broadcasted_iota(jnp.int32, (NODES, width), 1)

    def best_of(feat, gains):
        even, odd = left_acc[feat, :COLS], left_acc[feat, COLS:]
        left_odd = even + odd
        left_even = even + jnp.where(lane == 0, 0.0, pltpu.roll(odd, 1, axis=1))
        whole = jnp.broadcast_to(left_odd[:, HIGH - 1:], (COLS, HIGH))
        base = score(whole)
        gain = jnp.maximum(score(left_even) + score(whole - left_even) - base,
                           score(left_odd) + score(whole - left_odd) - base)
        best = jnp.max(gain, axis=1, keepdims=True)
        return jnp.where(gain_lane == me * own + feat,
                         jnp.broadcast_to(best, (NODES, width)), gains)

    gain_all[0] = lax.fori_loop(0, own, best_of, jnp.zeros((NODES, width), jnp.float32))

    @pl.loop(1, n)
    def _(k):
        gain_copy(k).start()

    @pl.loop(1, n)
    def _(k):
        gain_copy(k).wait_recv()

    out_ref[...] = jnp.sum(gain_all[...], axis=0)[:, :out_ref.shape[1]]

    @pl.loop(1, n)
    def _(k):
        stats_copy(k).wait_send()
        nodes_copy(k).wait_send()
        bins_copy(k).wait_send()
        gain_copy(k).wait_send()


def shards(bins, grads, hess, nodes, row_count):
    n = lax.axis_size("dp")
    feats, rows = bins.shape
    own = feats // n
    assert n & (n - 1) == 0 and own * n == feats
    width = -(-feats // LANES) * LANES
    vmem = pl.BlockSpec(memory_space=pltpu.VMEM)
    dma = pltpu.SemaphoreType.DMA
    return pl.pallas_call(
        functools.partial(kernel, n),
        out_shape=jax.ShapeDtypeStruct((NODES, feats), jnp.float32),
        in_specs=[pl.BlockSpec(memory_space=pl.ANY), vmem, vmem, vmem,
                  pl.BlockSpec(memory_space=pltpu.SMEM)],
        out_specs=vmem,
        scratch_shapes=[
            pltpu.VMEM((n, own, rows), jnp.int32),
            pltpu.VMEM((n, PAIR, rows), jnp.float32),
            pltpu.VMEM((n, 1, rows), jnp.int32),
            pltpu.VMEM((COLS, rows), jnp.bfloat16),
            pltpu.VMEM((own, 2 * COLS, HIGH), jnp.float32),
            pltpu.VMEM((n, NODES, width), jnp.float32),
            dma,
        ] + [dma((n,))] * 8,
        compiler_params=pltpu.CompilerParams(
            collective_id=0, has_side_effects=True, vmem_limit_bytes=40 << 20),
        name="histogram_gain",
    )(bins.reshape(n, own, rows), grads, hess, nodes.reshape(1, rows), row_count)


def solution(mesh):
    in_specs = (P("feat", "dp"), P(None, "dp"), P(None, "dp"), P("dp"), P("dp"))
    out_specs = P(None, "feat")
    return jax.shard_map(shards, mesh=mesh, in_specs=in_specs, out_specs=out_specs, check_vma=False)
```

```python
import functools
import math

import jax
import jax.numpy as jnp
from jax import lax
from jax.experimental import pallas as pl
from jax.experimental.pallas import tpu as pltpu
from jax.sharding import PartitionSpec as P

BINS = 256
OUT = 8
NODES = 4
PAIR = 2 * OUT
COLS = NODES * PAIR
HIGH = BINS // 2
LANES = 128
ROW_TILE = 512
OVER_LANES = (((1,), (1,)), ((), ()))


def score(sums):
    shaped = sums.reshape(NODES, PAIR, sums.shape[-1])
    grad_sum = shaped[:, :OUT, :]
    hess_sum = shaped[:, OUT:, :]
    return jnp.sum(grad_sum * grad_sum / (hess_sum + 1.0), axis=1)


def flip(index, k, size):
    other, bit = 0, 1
    while bit < size:
        other = other + ((index // bit + k // bit) % 2) * bit
        bit *= 2
    return other


def kernel(n, bins_ref, grads_ref, hess_ref, nodes_ref, count_ref, out_ref,
           bins_all, stats_all, weights, left_acc, gain_all,
           own_sem, bins_send, bins_recv, direct_send, pass_send, stats_recv,
           gain_send, gain_recv):
    own, rows = bins_all.shape[1:]
    parts = stats_all.shape[1]
    span = rows // parts
    me = lax.axis_index("dp")
    group = lax.axis_index("feat")
    my_part = group % parts

    def partner(k):
        return flip(me, k, n)

    def sibling(j):
        return group - my_part + flip(my_part, j, parts)

    def remote(src, dst, send, recv, dp, feat):
        return pltpu.make_async_remote_copy(
            src_ref=src, dst_ref=dst, send_sem=send, recv_sem=recv,
            device_id={"dp": dp, "feat": feat}, device_id_type=pl.DeviceIdType.MESH)

    def bins_copy(k):
        return remote(bins_ref.at[partner(k)], bins_all.at[k],
                      bins_send.at[k], bins_recv.at[k], partner(k), group)

    def gain_copy(k):
        return remote(gain_all.at[0], gain_all.at[k],
                      gain_send.at[k], gain_recv.at[k], partner(k), group)

    def pair_copy():
        return remote(stats_all.at[0], stats_all.at[1],
                      direct_send.at[1], stats_recv.at[1, 0], partner(1), group)

    def part_copy(k):
        return remote(stats_all.at[0, my_part], stats_all.at[k, my_part],
                      direct_send.at[k], stats_recv.at[k, 0], partner(k), group)

    def pass_copy(k, side, j):
        return remote(stats_all.at[k, my_part], stats_all.at[k + side, my_part],
                      pass_send.at[k, side, j], stats_recv.at[k + side, j],
                      partner(side), sibling(j))

    own_copy = pltpu.make_async_copy(bins_ref.at[me], bins_all.at[0], own_sem)
    own_copy.start()
    barrier = pltpu.get_barrier_semaphore()

    def greet(dp, feat):
        pl.semaphore_signal(barrier, inc=1, device_id={"dp": dp, "feat": feat},
                            device_id_type=pl.DeviceIdType.MESH)

    @pl.loop(1, n)
    def _(k):
        greet(partner(k), group)

    @pl.loop(1, parts)
    def _(j):
        greet(me, sibling(j))
        greet(partner(1), sibling(j))

    for part in range(parts):
        first = part * span
        stats_all[0, part, :OUT, :span] = grads_ref[:, first:first + span]
        stats_all[0, part, OUT:, :span] = hess_ref[:, first:first + span]
        for row in range(span // LANES):
            at = first + row * LANES
            slot_index = at + lax.broadcasted_iota(jnp.int32, (1, LANES), 1)
            stats_all[0, part, row:row + 1, span:] = jnp.where(
                slot_index < count_ref[0], nodes_ref[:, at:at + LANES],
                NODES).astype(jnp.float32)
        stats_all[0, part, span // LANES:, span:] = jnp.zeros(
            (PAIR - span // LANES, LANES), jnp.float32)
    pl.semaphore_wait(barrier, n - 1 + 2 * (parts - 1))

    pair_copy().start()

    @pl.loop(1, n // 2)
    def _(half):
        part_copy(2 * half).start()

    @pl.loop(1, n)
    def _(k):
        bins_copy(k).start()

    left_acc[...] = jnp.zeros_like(left_acc)
    own_copy.wait()

    @pl.loop(0, n)
    def _(k):
        @pl.when(k > 0)
        def _():
            bins_copy(k).wait_recv()

        @pl.when(k == 1)
        def _():
            pair_copy().wait_recv()

            @pl.loop(1, n // 2)
            def _(half):
                part_copy(2 * half).wait_recv()
                pass_copy(2 * half, 1, 0).start()

                @pl.loop(1, parts)
                def _(j):
                    pass_copy(2 * half, 0, j).start()
                    pass_copy(2 * half, 1, j).start()

        @pl.when(k > 1)
        def _():
            @pl.when(k % 2 == 1)
            def _():
                pass_copy(k - 1, 1, 0).wait_recv()

            @pl.loop(1, parts)
            def _(j):
                pass_copy(k - k % 2, k % 2, j).wait_recv()

        for part in range(parts):
            for row in range(span // LANES):
                block = slice(row * LANES, (row + 1) * LANES)
                stats = stats_all[k, part, :, block]
                label = jnp.broadcast_to(
                    stats_all[k, part, row:row + 1, span:], (PAIR, LANES))
                at = part * span + row * LANES
                for node in range(NODES):
                    weights[node * PAIR:(node + 1) * PAIR, at:at + LANES] = jnp.where(
                        label == node, stats, 0.0).astype(jnp.bfloat16)

        @pl.loop(0, own)
        def _(feat):
            total = None
            for start in range(0, rows, ROW_TILE):
                size = min(ROW_TILE, rows - start)
                code = bins_all[k, pl.ds(feat, 1), start:start + size]
                high = (code >> 1).astype(jnp.float32).astype(jnp.bfloat16)
                low = (code & 1).astype(jnp.float32).astype(jnp.bfloat16)
                levels = lax.broadcasted_iota(jnp.int32, (HIGH, size), 0)
                levels = levels.astype(jnp.float32).astype(jnp.bfloat16)
                below = jnp.where(jnp.broadcast_to(high, (HIGH, size)) <= levels,
                                  jnp.ones((), jnp.bfloat16), jnp.zeros((), jnp.bfloat16))
                whole = weights[:, start:start + size]
                odd = whole * jnp.broadcast_to(low, (COLS, size))
                both = jnp.concatenate([whole - odd, odd], axis=0)
                part = lax.dot_general(both, below, OVER_LANES,
                                       preferred_element_type=jnp.float32)
                total = part if total is None else total + part
            left_acc[feat] = left_acc[feat] + total

    lane = lax.broadcasted_iota(jnp.int32, (COLS, HIGH), 1)
    width = gain_all.shape[-1]
    gain_lane = lax.broadcasted_iota(jnp.int32, (NODES, width), 1)

    def best_of(feat, gains):
        even, odd = left_acc[feat, :COLS], left_acc[feat, COLS:]
        left_odd = even + odd
        left_even = even + jnp.where(lane == 0, 0.0, pltpu.roll(odd, 1, axis=1))
        whole = jnp.broadcast_to(left_odd[:, HIGH - 1:], (COLS, HIGH))
        base = score(whole)
        gain = jnp.maximum(score(left_even) + score(whole - left_even) - base,
                           score(left_odd) + score(whole - left_odd) - base)
        best = jnp.max(gain, axis=1, keepdims=True)
        return jnp.where(gain_lane == me * own + feat,
                         jnp.broadcast_to(best, (NODES, width)), gains)

    gain_all[0] = lax.fori_loop(0, own, best_of, jnp.zeros((NODES, width), jnp.float32))

    @pl.loop(1, n)
    def _(k):
        gain_copy(k).start()

    @pl.loop(1, n)
    def _(k):
        gain_copy(k).wait_recv()

    out_ref[...] = jnp.sum(gain_all[...], axis=0)[:, :out_ref.shape[1]]

    pair_copy().wait_send()

    @pl.loop(1, n // 2)
    def _(half):
        part_copy(2 * half).wait_send()
        pass_copy(2 * half, 1, 0).wait_send()

        @pl.loop(1, parts)
        def _(j):
            pass_copy(2 * half, 0, j).wait_send()
            pass_copy(2 * half, 1, j).wait_send()

    @pl.loop(1, n)
    def _(k):
        bins_copy(k).wait_send()
        gain_copy(k).wait_send()


def shards(bins, grads, hess, nodes, row_count):
    n = lax.axis_size("dp")
    feats, rows = bins.shape
    own = feats // n
    assert n & (n - 1) == 0 and own * n == feats
    parts = math.gcd(lax.axis_size("feat"), rows // LANES)
    assert n > 1 and parts & (parts - 1) == 0 and rows % (parts * LANES) == 0
    width = -(-feats // LANES) * LANES
    vmem = pl.BlockSpec(memory_space=pltpu.VMEM)
    dma = pltpu.SemaphoreType.DMA
    return pl.pallas_call(
        functools.partial(kernel, n),
        out_shape=jax.ShapeDtypeStruct((NODES, feats), jnp.float32),
        in_specs=[pl.BlockSpec(memory_space=pl.ANY), vmem, vmem, vmem,
                  pl.BlockSpec(memory_space=pltpu.SMEM)],
        out_specs=vmem,
        scratch_shapes=[
            pltpu.VMEM((n, own, rows), jnp.int32),
            pltpu.VMEM((n, parts, PAIR, rows // parts + LANES), jnp.float32),
            pltpu.VMEM((COLS, rows), jnp.bfloat16),
            pltpu.VMEM((own, 2 * COLS, HIGH), jnp.float32),
            pltpu.VMEM((n, NODES, width), jnp.float32),
            dma, dma((n,)), dma((n,)), dma((n,)), dma((n, 2, parts)), dma((n, parts)),
            dma((n,)), dma((n,)),
        ],
        compiler_params=pltpu.CompilerParams(
            collective_id=0, has_side_effects=True, vmem_limit_bytes=40 << 20),
        name="histogram_gain",
    )(bins.reshape(n, own, rows), grads, hess, nodes.reshape(1, rows), row_count)


def solution(mesh):
    in_specs = (P("feat", "dp"), P(None, "dp"), P(None, "dp"), P("dp"), P("dp"))
    out_specs = P(None, "feat")
    return jax.shard_map(shards, mesh=mesh, in_specs=in_specs, out_specs=out_specs, check_vma=False)
```

```python
import functools
import math

import jax
import jax.numpy as jnp
from jax import lax
from jax.experimental import pallas as pl
from jax.experimental.pallas import tpu as pltpu
from jax.sharding import PartitionSpec as P

BINS = 256
OUT = 8
NODES = 4
PAIR = 2 * OUT
COLS = NODES * PAIR
HIGH = BINS // 2
LANES = 128
ROW_TILE = 512
OVER_LANES = (((1,), (1,)), ((), ()))


def score(sums):
    shaped = sums.reshape(NODES, PAIR, sums.shape[-1])
    grad_sum = shaped[:, :OUT, :]
    hess_sum = shaped[:, OUT:, :]
    return jnp.sum(grad_sum * grad_sum / (hess_sum + 1.0), axis=1)


def flip(index, k, size):
    other, bit = 0, 1
    while bit < size:
        other = other + ((index // bit + k // bit) % 2) * bit
        bit *= 2
    return other


def kernel(n, bins_ref, grads_ref, hess_ref, nodes_ref, count_ref, out_ref,
           bins_all, stats_all, weights, left_acc, gain_all,
           own_sem, bins_send, bins_recv, direct_send, pass_send, stats_recv,
           gain_send, gain_recv):
    own, rows = bins_all.shape[1:]
    parts = stats_all.shape[1]
    span = rows // parts
    me = lax.axis_index("dp")
    group = lax.axis_index("feat")
    my_part = group % parts

    def partner(k):
        return flip(me, k, n)

    def sibling(j):
        return group - my_part + flip(my_part, j, parts)

    def remote(src, dst, send, recv, dp, feat):
        return pltpu.make_async_remote_copy(
            src_ref=src, dst_ref=dst, send_sem=send, recv_sem=recv,
            device_id={"dp": dp, "feat": feat}, device_id_type=pl.DeviceIdType.MESH)

    def bins_copy(k):
        return remote(bins_ref.at[partner(k)], bins_all.at[k],
                      bins_send.at[k], bins_recv.at[k], partner(k), group)

    def gain_copy(k):
        return remote(gain_all.at[0], gain_all.at[k],
                      gain_send.at[k], gain_recv.at[k], partner(k), group)

    def pair_copy():
        return remote(stats_all.at[0], stats_all.at[1],
                      direct_send.at[1], stats_recv.at[1, 0], partner(1), group)

    def part_copy(k):
        return remote(stats_all.at[0, my_part], stats_all.at[k, my_part],
                      direct_send.at[k], stats_recv.at[k, 0], partner(k), group)

    def pass_copy(k, side, j):
        return remote(stats_all.at[k, my_part], stats_all.at[k + side, my_part],
                      pass_send.at[k, side, j], stats_recv.at[k + side, j],
                      partner(side), sibling(j))

    own_copy = pltpu.make_async_copy(bins_ref.at[me], bins_all.at[0], own_sem)
    own_copy.start()
    barrier = pltpu.get_barrier_semaphore()

    def greet(dp, feat):
        pl.semaphore_signal(barrier, inc=1, device_id={"dp": dp, "feat": feat},
                            device_id_type=pl.DeviceIdType.MESH)

    @pl.loop(1, n)
    def _(k):
        greet(partner(k), group)

    @pl.loop(1, parts)
    def _(j):
        greet(me, sibling(j))
        greet(partner(1), sibling(j))

    for part in range(parts):
        first = part * span
        stats_all[0, part, :OUT, :span] = grads_ref[:, first:first + span]
        stats_all[0, part, OUT:, :span] = hess_ref[:, first:first + span]
        for row in range(span // LANES):
            at = first + row * LANES
            slot_index = at + lax.broadcasted_iota(jnp.int32, (1, LANES), 1)
            stats_all[0, part, row:row + 1, span:] = jnp.where(
                slot_index < count_ref[0], nodes_ref[:, at:at + LANES],
                NODES).astype(jnp.float32)
        stats_all[0, part, span // LANES:, span:] = jnp.zeros(
            (PAIR - span // LANES, LANES), jnp.float32)
    pl.semaphore_wait(barrier, n - 1 + 2 * (parts - 1))

    pair_copy().start()

    @pl.loop(1, n // 2)
    def _(half):
        part_copy(2 * half).start()

    @pl.loop(1, n)
    def _(k):
        bins_copy(k).start()

    left_acc[...] = jnp.zeros_like(left_acc)
    own_copy.wait()

    @pl.loop(0, n)
    def _(k):
        @pl.when(k > 0)
        def _():
            bins_copy(k).wait_recv()

        @pl.when(k == 1)
        def _():
            pair_copy().wait_recv()

            @pl.loop(1, n // 2)
            def _(half):
                part_copy(2 * half).wait_recv()
                pass_copy(2 * half, 1, 0).start()

                @pl.loop(1, parts)
                def _(j):
                    pass_copy(2 * half, 0, j).start()
                    pass_copy(2 * half, 1, j).start()

        @pl.when(k > 1)
        def _():
            @pl.when(k % 2 == 1)
            def _():
                pass_copy(k - 1, 1, 0).wait_recv()

            @pl.loop(1, parts)
            def _(j):
                pass_copy(k - k % 2, k % 2, j).wait_recv()

        for part in range(parts):
            for row in range(span // LANES):
                block = slice(row * LANES, (row + 1) * LANES)
                stats = stats_all[k, part, :, block]
                label = jnp.broadcast_to(
                    stats_all[k, part, row:row + 1, span:], (PAIR, LANES))
                at = part * span + row * LANES
                for node in range(NODES):
                    weights[node * PAIR:(node + 1) * PAIR, at:at + LANES] = jnp.where(
                        label == node, stats, 0.0).astype(jnp.bfloat16)

        @pl.loop(0, own, unroll=min(own, 8))
        def _(feat):
            total = None
            for start in range(0, rows, ROW_TILE):
                size = min(ROW_TILE, rows - start)
                code = bins_all[k, pl.ds(feat, 1), start:start + size]
                high = (code >> 1).astype(jnp.float32).astype(jnp.bfloat16)
                low = (code & 1).astype(jnp.float32).astype(jnp.bfloat16)
                levels = lax.broadcasted_iota(jnp.int32, (HIGH, size), 0)
                levels = levels.astype(jnp.float32).astype(jnp.bfloat16)
                below = jnp.where(jnp.broadcast_to(high, (HIGH, size)) <= levels,
                                  jnp.ones((), jnp.bfloat16), jnp.zeros((), jnp.bfloat16))
                whole = weights[:, start:start + size]
                odd = whole * jnp.broadcast_to(low, (COLS, size))
                both = jnp.concatenate([whole - odd, odd], axis=0)
                part = lax.dot_general(both, below, OVER_LANES,
                                       preferred_element_type=jnp.float32)
                total = part if total is None else total + part
            left_acc[feat] = left_acc[feat] + total

    lane = lax.broadcasted_iota(jnp.int32, (COLS, HIGH), 1)
    width = gain_all.shape[-1]
    gain_lane = lax.broadcasted_iota(jnp.int32, (NODES, width), 1)

    def best_of(feat, gains):
        even, odd = left_acc[feat, :COLS], left_acc[feat, COLS:]
        left_odd = even + odd
        left_even = even + jnp.where(lane == 0, 0.0, pltpu.roll(odd, 1, axis=1))
        whole = jnp.broadcast_to(left_odd[:, HIGH - 1:], (COLS, HIGH))
        base = score(whole)
        gain = jnp.maximum(score(left_even) + score(whole - left_even) - base,
                           score(left_odd) + score(whole - left_odd) - base)
        best = jnp.max(gain, axis=1, keepdims=True)
        return jnp.where(gain_lane == me * own + feat,
                         jnp.broadcast_to(best, (NODES, width)), gains)

    gain_all[0] = lax.fori_loop(0, own, best_of, jnp.zeros((NODES, width), jnp.float32), unroll=min(own, 4))

    @pl.loop(1, n)
    def _(k):
        gain_copy(k).start()

    @pl.loop(1, n)
    def _(k):
        gain_copy(k).wait_recv()

    out_ref[...] = jnp.sum(gain_all[...], axis=0)[:, :out_ref.shape[1]]

    pair_copy().wait_send()

    @pl.loop(1, n // 2)
    def _(half):
        part_copy(2 * half).wait_send()
        pass_copy(2 * half, 1, 0).wait_send()

        @pl.loop(1, parts)
        def _(j):
            pass_copy(2 * half, 0, j).wait_send()
            pass_copy(2 * half, 1, j).wait_send()

    @pl.loop(1, n)
    def _(k):
        bins_copy(k).wait_send()
        gain_copy(k).wait_send()


def shards(bins, grads, hess, nodes, row_count):
    n = lax.axis_size("dp")
    feats, rows = bins.shape
    own = feats // n
    assert n & (n - 1) == 0 and own * n == feats
    parts = math.gcd(lax.axis_size("feat"), rows // LANES)
    assert n > 1 and parts & (parts - 1) == 0 and rows % (parts * LANES) == 0
    width = -(-feats // LANES) * LANES
    vmem = pl.BlockSpec(memory_space=pltpu.VMEM)
    dma = pltpu.SemaphoreType.DMA
    return pl.pallas_call(
        functools.partial(kernel, n),
        out_shape=jax.ShapeDtypeStruct((NODES, feats), jnp.float32),
        in_specs=[pl.BlockSpec(memory_space=pl.ANY), vmem, vmem, vmem,
                  pl.BlockSpec(memory_space=pltpu.SMEM)],
        out_specs=vmem,
        scratch_shapes=[
            pltpu.VMEM((n, own, rows), jnp.int32),
            pltpu.VMEM((n, parts, PAIR, rows // parts + LANES), jnp.float32),
            pltpu.VMEM((COLS, rows), jnp.bfloat16),
            pltpu.VMEM((own, 2 * COLS, HIGH), jnp.float32),
            pltpu.VMEM((n, NODES, width), jnp.float32),
            dma, dma((n,)), dma((n,)), dma((n,)), dma((n, 2, parts)), dma((n, parts)),
            dma((n,)), dma((n,)),
        ],
        compiler_params=pltpu.CompilerParams(
            collective_id=0, has_side_effects=True, vmem_limit_bytes=40 << 20),
        name="histogram_gain",
    )(bins.reshape(n, own, rows), grads, hess, nodes.reshape(1, rows), row_count)


def solution(mesh):
    in_specs = (P("feat", "dp"), P(None, "dp"), P(None, "dp"), P("dp"), P("dp"))
    out_specs = P(None, "feat")
    return jax.shard_map(shards, mesh=mesh, in_specs=in_specs, out_specs=out_specs, check_vma=False)
```

```python
import functools
import math

import jax
import jax.numpy as jnp
from jax import lax
from jax.experimental import pallas as pl
from jax.experimental.pallas import tpu as pltpu
from jax.sharding import PartitionSpec as P

BINS = 256
OUT = 8
NODES = 4
PAIR = 2 * OUT
COLS = NODES * PAIR
HIGH = BINS // 2
LANES = 128
ROW_TILE = 512
OVER_LANES = (((1,), (1,)), ((), ()))


def score(sums):
    shaped = sums.reshape(NODES, PAIR, sums.shape[-1])
    grad_sum = shaped[:, :OUT, :]
    hess_sum = shaped[:, OUT:, :]
    return jnp.sum(grad_sum * grad_sum / (hess_sum + 1.0), axis=1)


def flip(index, k, size):
    other, bit = 0, 1
    while bit < size:
        other = other + ((index // bit + k // bit) % 2) * bit
        bit *= 2
    return other


def kernel(n, bins_ref, grads_ref, hess_ref, nodes_ref, count_ref, out_ref,
           bins_all, stats_all, weights, left_acc, gain_all,
           own_sem, bins_send, bins_recv, direct_send, pass_send, stats_recv,
           gain_send, gain_recv):
    own, rows = bins_all.shape[1:]
    parts = stats_all.shape[1]
    halves = bins_send.shape[1]
    span = rows // parts
    me = lax.axis_index("dp")
    group = lax.axis_index("feat")
    my_part = group % parts

    def partner(k):
        return flip(me, k, n)

    def sibling(j):
        return group - my_part + flip(my_part, j, parts)

    def remote(src, dst, send, recv, dp, feat):
        return pltpu.make_async_remote_copy(
            src_ref=src, dst_ref=dst, send_sem=send, recv_sem=recv,
            device_id={"dp": dp, "feat": feat}, device_id_type=pl.DeviceIdType.MESH)

    def bins_copy(k, half):
        some = pl.ds(half * (own // halves), own // halves)
        return remote(bins_ref.at[partner(k), some], bins_all.at[k, some],
                      bins_send.at[k, half], bins_recv.at[k, half], partner(k), group)

    def gain_copy(k):
        return remote(gain_all.at[0], gain_all.at[k],
                      gain_send.at[k], gain_recv.at[k], partner(k), group)

    def pair_copy():
        return remote(stats_all.at[0], stats_all.at[1],
                      direct_send.at[1], stats_recv.at[1, 0], partner(1), group)

    def part_copy(k):
        return remote(stats_all.at[0, my_part], stats_all.at[k, my_part],
                      direct_send.at[k], stats_recv.at[k, 0], partner(k), group)

    def pass_copy(k, side, j):
        return remote(stats_all.at[k, my_part], stats_all.at[k + side, my_part],
                      pass_send.at[k, side, j], stats_recv.at[k + side, j],
                      partner(side), sibling(j))

    own_copy = pltpu.make_async_copy(bins_ref.at[me], bins_all.at[0], own_sem)
    own_copy.start()
    barrier = pltpu.get_barrier_semaphore()

    def greet(dp, feat):
        pl.semaphore_signal(barrier, inc=1, device_id={"dp": dp, "feat": feat},
                            device_id_type=pl.DeviceIdType.MESH)

    @pl.loop(1, n)
    def _(k):
        greet(partner(k), group)

    @pl.loop(1, parts)
    def _(j):
        greet(me, sibling(j))
        greet(partner(1), sibling(j))

    for part in range(parts):
        first = part * span
        stats_all[0, part, :OUT, :span] = grads_ref[:, first:first + span]
        stats_all[0, part, OUT:, :span] = hess_ref[:, first:first + span]
        for row in range(span // LANES):
            at = first + row * LANES
            slot_index = at + lax.broadcasted_iota(jnp.int32, (1, LANES), 1)
            stats_all[0, part, row:row + 1, span:] = jnp.where(
                slot_index < count_ref[0], nodes_ref[:, at:at + LANES],
                NODES).astype(jnp.float32)
        stats_all[0, part, span // LANES:, span:] = jnp.zeros(
            (PAIR - span // LANES, LANES), jnp.float32)
    pl.semaphore_wait(barrier, n - 1 + 2 * (parts - 1))

    pair_copy().start()

    @pl.loop(1, n // 2)
    def _(half):
        part_copy(2 * half).start()

    @pl.loop(1, n)
    def _(k):
        for half in range(halves):
            bins_copy(k, half).start()

    left_acc[...] = jnp.zeros_like(left_acc)
    own_copy.wait()

    @pl.loop(0, n)
    def _(k):
        @pl.when(k == 1)
        def _():
            pair_copy().wait_recv()

            @pl.loop(1, n // 2)
            def _(half):
                part_copy(2 * half).wait_recv()
                pass_copy(2 * half, 1, 0).start()

                @pl.loop(1, parts)
                def _(j):
                    pass_copy(2 * half, 0, j).start()
                    pass_copy(2 * half, 1, j).start()

        @pl.when(k > 1)
        def _():
            @pl.when(k % 2 == 1)
            def _():
                pass_copy(k - 1, 1, 0).wait_recv()

            @pl.loop(1, parts)
            def _(j):
                pass_copy(k - k % 2, k % 2, j).wait_recv()

        for part in range(parts):
            for row in range(span // LANES):
                block = slice(row * LANES, (row + 1) * LANES)
                stats = stats_all[k, part, :, block]
                label = jnp.broadcast_to(
                    stats_all[k, part, row:row + 1, span:], (PAIR, LANES))
                at = part * span + row * LANES
                for node in range(NODES):
                    weights[node * PAIR:(node + 1) * PAIR, at:at + LANES] = jnp.where(
                        label == node, stats, 0.0).astype(jnp.bfloat16)

        @pl.loop(0, halves)
        def _(half):
            @pl.when(k > 0)
            def _():
                bins_copy(k, half).wait_recv()

            @pl.loop(0, own // halves, unroll=min(own // halves, 8))
            def _(at):
                feat = half * (own // halves) + at
                total = None
                for start in range(0, rows, ROW_TILE):
                    size = min(ROW_TILE, rows - start)
                    code = bins_all[k, pl.ds(feat, 1), start:start + size]
                    high = (code >> 1).astype(jnp.float32).astype(jnp.bfloat16)
                    low = (code & 1).astype(jnp.float32).astype(jnp.bfloat16)
                    levels = lax.broadcasted_iota(jnp.int32, (HIGH, size), 0)
                    levels = levels.astype(jnp.float32).astype(jnp.bfloat16)
                    below = jnp.where(jnp.broadcast_to(high, (HIGH, size)) <= levels,
                                      jnp.ones((), jnp.bfloat16), jnp.zeros((), jnp.bfloat16))
                    whole = weights[:, start:start + size]
                    odd = whole * jnp.broadcast_to(low, (COLS, size))
                    both = jnp.concatenate([whole - odd, odd], axis=0)
                    part = lax.dot_general(both, below, OVER_LANES,
                                           preferred_element_type=jnp.float32)
                    total = part if total is None else total + part
                left_acc[feat] = left_acc[feat] + total

    lane = lax.broadcasted_iota(jnp.int32, (COLS, HIGH), 1)
    width = gain_all.shape[-1]
    gain_lane = lax.broadcasted_iota(jnp.int32, (NODES, width), 1)

    def best_of(feat, gains):
        even, odd = left_acc[feat, :COLS], left_acc[feat, COLS:]
        left_odd = even + odd
        left_even = even + jnp.where(lane == 0, 0.0, pltpu.roll(odd, 1, axis=1))
        whole = jnp.broadcast_to(left_odd[:, HIGH - 1:], (COLS, HIGH))
        base = score(whole)
        gain = jnp.maximum(score(left_even) + score(whole - left_even) - base,
                           score(left_odd) + score(whole - left_odd) - base)
        best = jnp.max(gain, axis=1, keepdims=True)
        return jnp.where(gain_lane == me * own + feat,
                         jnp.broadcast_to(best, (NODES, width)), gains)

    gain_all[0] = lax.fori_loop(0, own, best_of, jnp.zeros((NODES, width), jnp.float32), unroll=min(own, 4))

    @pl.loop(1, n)
    def _(k):
        gain_copy(k).start()

    @pl.loop(1, n)
    def _(k):
        gain_copy(k).wait_recv()

    out_ref[...] = jnp.sum(gain_all[...], axis=0)[:, :out_ref.shape[1]]

    pair_copy().wait_send()

    @pl.loop(1, n // 2)
    def _(half):
        part_copy(2 * half).wait_send()
        pass_copy(2 * half, 1, 0).wait_send()

        @pl.loop(1, parts)
        def _(j):
            pass_copy(2 * half, 0, j).wait_send()
            pass_copy(2 * half, 1, j).wait_send()

    @pl.loop(1, n)
    def _(k):
        for half in range(halves):
            bins_copy(k, half).wait_send()
        gain_copy(k).wait_send()


def shards(bins, grads, hess, nodes, row_count):
    n = lax.axis_size("dp")
    feats, rows = bins.shape
    own = feats // n
    assert n & (n - 1) == 0 and own * n == feats
    parts = math.gcd(lax.axis_size("feat"), rows // LANES)
    assert n > 1 and parts & (parts - 1) == 0 and rows % (parts * LANES) == 0
    halves = 2 if own % 16 == 0 else 1
    width = -(-feats // LANES) * LANES
    vmem = pl.BlockSpec(memory_space=pltpu.VMEM)
    dma = pltpu.SemaphoreType.DMA
    return pl.pallas_call(
        functools.partial(kernel, n),
        out_shape=jax.ShapeDtypeStruct((NODES, feats), jnp.float32),
        in_specs=[pl.BlockSpec(memory_space=pl.ANY), vmem, vmem, vmem,
                  pl.BlockSpec(memory_space=pltpu.SMEM)],
        out_specs=vmem,
        scratch_shapes=[
            pltpu.VMEM((n, own, rows), jnp.int32),
            pltpu.VMEM((n, parts, PAIR, rows // parts + LANES), jnp.float32),
            pltpu.VMEM((COLS, rows), jnp.bfloat16),
            pltpu.VMEM((own, 2 * COLS, HIGH), jnp.float32),
            pltpu.VMEM((n, NODES, width), jnp.float32),
            dma, dma((n, halves)), dma((n, halves)), dma((n,)), dma((n, 2, parts)), dma((n, parts)),
            dma((n,)), dma((n,)),
        ],
        compiler_params=pltpu.CompilerParams(
            collective_id=0, has_side_effects=True, vmem_limit_bytes=40 << 20),
        name="histogram_gain",
    )(bins.reshape(n, own, rows), grads, hess, nodes.reshape(1, rows), row_count)


def solution(mesh):
    in_specs = (P("feat", "dp"), P(None, "dp"), P(None, "dp"), P("dp"), P("dp"))
    out_specs = P(None, "feat")
    return jax.shard_map(shards, mesh=mesh, in_specs=in_specs, out_specs=out_specs, check_vma=False)
```
